32 devices in a mesh: lat: 8 (over z, core), depth: 4 (over y, x).
Axes of the slice: x: 2, y: 2, z: 4, core: 2. Of those that a mesh axis runs over, the one named last changes fastest.
Arguments:
- volume: float32 [16, 256, 2048], P('depth', 'lat'), may hold values from -6 to 6
- measured: float32 [4, 128, 2048], P('depth', 'lat'), may hold values from -12 to 12
- kernels: bfloat16 [4, 128, 128], replicated, may hold values from -0.5 to 0.5
- src_block: int32 [4, 8, 4, 1024], P('depth', 'lat'), may hold values from 0 to 2047
- dst_block: int32 [4, 8, 4, 1024], P('depth', 'lat'), may hold values from 0 to 255
- path_weight: float32 [4, 8, 4, 1024], P('depth', 'lat'), may hold values from 0.1 to 1
- block_counts: int32 [4, 8, 4], P('depth', 'lat'), may hold values from 128 to 1024, as said below
Outputs:
- updated: float32 [16, 256, 2048], P('depth', 'lat')
- residual: float32 [4, 128, 2048], P('depth', 'lat')
The draws below stay inside these ranges and needn't reach their ends.
Inputs may be any that keep to these rules, and one draw needn't show every extreme that they name: Only the first block_counts entries of a list are live; in every draw some slab, tile and angle has all 1024 entries live.
All inputs are finite; a program needn't handle non-finite values.
Results may differ from the reference program's by a relative error of at most 0.0026.
Values may be sent and summed in bfloat16 or wider, within the bound.
A program may use at most 64 MiB of HBM per device.

```python
import math
import jax
import jax.numpy as jnp
from jax import lax

DZ = 4
RW = 32
COLS = 2048
BLK = 128
DR = 16
DCOL = 2048
CAP = 1024
SLABS = 4
TILES = 8
NA = 4
NB = 2048
DB = 256


def draw_block_counts(key, part):
    key_level = jax.random.fold_in(key, 11)
    key_base = jax.random.fold_in(key, 12)
    key_spot = jax.random.fold_in(key, 13)
    shifts = jax.random.randint(key_level, (1, TILES, 1), 0, 3)
    levels = jnp.left_shift(jnp.ones((1, TILES, 1), jnp.int32), shifts)
    base_counts = jax.random.randint(key_base, (SLABS, TILES, NA), CAP // 8, CAP // 4 + 1)
    counts = jnp.minimum(base_counts * levels, CAP).reshape(-1)
    chosen = jax.random.randint(key_spot, (), 0, SLABS * TILES * NA)
    counts = counts.at[chosen].set(CAP)
    return counts.reshape(SLABS, TILES, NA).astype(jnp.int32)


def touch_ends(values, stream_key, least, top_value):
    place = [jax.random.randint(jax.random.fold_in(stream_key, axis), (), 0, length) for axis, length in enumerate(values.shape)]
    main_axis = values.shape.index(max(values.shape))
    next_to = place[:main_axis] + [(place[main_axis] + 1) % values.shape[main_axis]] + place[main_axis + 1:]
    return values.at[tuple(place)].set(least).at[tuple(next_to)].set(top_value)


def block_scale(rng, dims, cuts, least, high):
    def one(dim, parts):
        heights = jax.random.uniform(jax.random.fold_in(jax.random.fold_in(rng, 6), dim), (parts,), jnp.float32, least / len(cuts), high / len(cuts))
        return jnp.repeat(jnp.exp(heights), dims[dim] // parts).reshape((-1,) + (1,) * (len(dims) - dim - 1))

    loudness = one(*cuts[0])
    for cut in cuts[1:]:
        loudness = loudness * one(*cut)
    return loudness


def centred(rng, extent, scale, reach, cuts=(), kind=jnp.bfloat16):
    array = scale * jax.random.normal(rng, extent, jnp.float32)
    if cuts:
        array = array * block_scale(rng, extent, cuts, -0.22, 0.18)
    return jnp.clip(array, -reach, reach).astype(kind)


def setup_inputs(seed: int = 0) -> dict:
    splits = jax.random.split(jax.random.key(seed), 8)
    volume = centred(splits[0], (DZ * SLABS, RW * TILES, COLS), 1.0, 6.0, ((0, 4), (1, 8)), jnp.float32)
    measured = centred(splits[1], (NA, DR * TILES, DCOL), 2.0, 12.0, ((0, 4), (1, 8)), jnp.float32)
    kernels = centred(splits[2], (NA, BLK, BLK), BLK ** -0.5, 0.5)
    src_block = touch_ends(jax.random.randint(splits[3], (SLABS, TILES, NA, CAP), 0, NB), jax.random.fold_in(splits[3], 1), 0, NB - 1).astype(jnp.int32)
    dst_block = touch_ends(jax.random.randint(splits[4], (SLABS, TILES, NA, CAP), 0, DB), jax.random.fold_in(splits[4], 1), 0, DB - 1).astype(jnp.int32)
    path_weight = jnp.clip(jnp.exp(math.log(1.0) - 2.3025851 * jax.random.uniform(splits[5], (SLABS, TILES, NA, CAP), jnp.float32) ** block_scale(splits[5], (SLABS, TILES, NA, CAP), ((0, 4), (1, 8)), -0.2, 0.2)), 0.1, 1.0)
    block_counts = draw_block_counts(jax.random.fold_in(splits[7], 71), 0)
    return dict(volume=volume, measured=measured, kernels=kernels, src_block=src_block, dst_block=dst_block, path_weight=path_weight, block_counts=block_counts)


SMOOTH_EPS = 0.1
STEP_SIZE = 0.1
TV_WEIGHT = 0.5

def slope_of(change):
    return change * lax.rsqrt(change * change + SMOOTH_EPS * SMOOTH_EPS)

def gather_rows(blocks, indices):
    return jnp.take(blocks, indices, axis=0)

def bucket_sum(values, indices):
    return jax.ops.segment_sum(values, indices, num_segments=DB)

def reference(volume, measured, kernels, src_block, dst_block, path_weight, block_counts):
    vol_b = volume.astype(jnp.bfloat16)
    active = (jnp.arange(CAP, dtype=jnp.int32)[None, None, None, :] < block_counts[..., None]).astype(jnp.float32)
    scales = path_weight * active
    kernel_f = kernels.astype(jnp.float32)

    def tile_blocks(slab_idx):
        slab_vol = lax.dynamic_slice_in_dim(vol_b, slab_idx * DZ, DZ, 0)
        return slab_vol.reshape(DZ, TILES, RW, COLS).transpose(1, 0, 2, 3).reshape(TILES, NB, BLK)

    def slab_forward(running, slab_idx):
        blocks = tile_blocks(slab_idx)
        picked = jax.vmap(gather_rows)(blocks, src_block[slab_idx])
        scaled = (picked.astype(jnp.float32) * scales[slab_idx][..., None]).astype(jnp.bfloat16)
        scaled = lax.optimization_barrier(scaled).astype(jnp.float32)
        summed = jax.vmap(jax.vmap(bucket_sum))(scaled, dst_block[slab_idx]).astype(jnp.bfloat16)
        summed = lax.optimization_barrier(summed).astype(jnp.float32)
        term = jnp.einsum('tadk,akj->tadj', summed, kernel_f, precision=lax.Precision.HIGHEST)
        return (running + term, None)
    start_sum = jnp.zeros((TILES, NA, DB, BLK), jnp.float32)
    projected, _ = lax.scan(slab_forward, start_sum, jnp.arange(SLABS, dtype=jnp.int32))
    projected = projected.transpose(1, 0, 2, 3).reshape(NA, TILES * DR, DCOL)
    residual = projected - measured
    back = lax.optimization_barrier(residual.astype(jnp.bfloat16)).astype(jnp.float32)
    back = back.reshape(NA, TILES, DB, BLK).transpose(1, 0, 2, 3)
    back_rows = jnp.einsum('tadj,akj->tadk', back, kernel_f, precision=lax.Precision.HIGHEST).astype(jnp.bfloat16)
    back_rows = lax.optimization_barrier(back_rows).astype(jnp.float32)

    def tile_sum(values, indices):
        return jax.ops.segment_sum(values.reshape(NA * CAP, BLK), indices.reshape(NA * CAP), num_segments=NB)

    def slab_adjoint(slab_idx):
        picked = jax.vmap(jax.vmap(gather_rows))(back_rows, dst_block[slab_idx])
        weighted = picked * scales[slab_idx][..., None]
        grads = jax.vmap(tile_sum)(weighted, src_block[slab_idx])
        return grads.reshape(TILES, DZ, RW, COLS).transpose(1, 0, 2, 3).reshape(DZ, TILES * RW, COLS)
    adjoint = lax.map(slab_adjoint, jnp.arange(SLABS, dtype=jnp.int32)).reshape(volume.shape)
    padded = jnp.pad(volume, 1)
    smooth = slope_of(volume - padded[:-2, 1:-1, 1:-1]) - slope_of(padded[2:, 1:-1, 1:-1] - volume)
    smooth = smooth + slope_of(volume - padded[1:-1, :-2, 1:-1]) - slope_of(padded[1:-1, 2:, 1:-1] - volume)
    smooth = smooth + slope_of(volume - padded[1:-1, 1:-1, :-2]) - slope_of(padded[1:-1, 1:-1, 2:] - volume)
    updated = volume - STEP_SIZE * (adjoint + TV_WEIGHT * smooth)
    return (updated, residual)
```

```python
import functools

import jax
import jax.numpy as jnp
from jax import lax
from jax.experimental import pallas as pl
from jax.experimental.pallas import tpu as pltpu
from jax.sharding import PartitionSpec as P

SMOOTH_EPS = 0.1
STEP_SIZE = 0.1
TV_WEIGHT = 0.5
F32 = jnp.float32
BF16 = jnp.bfloat16
MESH = pl.DeviceIdType.MESH
NT = (((1,), (1,)), ((), ()))
PAD = 8


def slope_of(change):
    return change * lax.rsqrt(change * change + SMOOTH_EPS * SMOOTH_EPS)


def body(
    vol_hbm, meas_ref, kern_ref, src_ref, dst_ref, weight_ref, count_ref,
    out_hbm, res_ref,
    vpad, vol_t, lo_hot, det_hot, gsend, gbuf, bbuf, wide, adj_t, pre, outv,
    hz_send, hz_recv, hy_send, hy_recv,
    in_sem, out_sem, gs_sem, gr_sem, bs_sem, br_sem, hzs_sem, hzr_sem, hys_sem, hyr_sem,
):
    n = lax.axis_size("depth")
    lats = lax.axis_size("lat")
    me = lax.axis_index("depth")
    lat = lax.axis_index("lat")
    zs, ys, xs = outv.shape
    zy = zs * ys
    own, rows, _ = meas_ref.shape
    width = kern_ref.shape[1]
    cols = xs // width
    cap = src_ref.shape[1]
    lo_size = lo_hot.shape[1]
    group = lo_size // zy
    heights = cols // group
    dets = det_hot.shape[1]
    step = min(256, cap)
    tiles = cap // step

    load = pltpu.make_async_copy(vol_hbm, vpad.at[pl.ds(1, zs), pl.ds(PAD, ys), :], in_sem)
    load.start()
    barrier = pltpu.get_barrier_semaphore()

    @pl.loop(1, n)
    def _(s):
        peer = lax.rem(me + s, n)
        pl.semaphore_signal(barrier, inc=1, device_id={"depth": peer}, device_id_type=MESH)

    @pl.when(lat > 0)
    def _():
        pl.semaphore_signal(barrier, inc=1, device_id={"lat": lat - 1}, device_id_type=MESH)

    @pl.when(lat < lats - 1)
    def _():
        pl.semaphore_signal(barrier, inc=1, device_id={"lat": lat + 1}, device_id_type=MESH)

    load.wait()
    hz_send[0] = vpad[1, pl.ds(PAD, ys), :].astype(BF16)
    hz_send[1] = vpad[zs, pl.ds(PAD, ys), :].astype(BF16)
    hy_send[0] = vpad[pl.ds(1, zs), PAD, :].astype(BF16)
    hy_send[1] = vpad[pl.ds(1, zs), PAD + ys - 1, :].astype(BF16)

    beside = (lat > 0).astype(jnp.int32) + (lat < lats - 1).astype(jnp.int32)
    pl.semaphore_wait(barrier, n - 1 + beside)

    def z_copy(part, peer):
        return pltpu.make_async_remote_copy(
            src_ref=hz_send.at[part], dst_ref=hz_recv.at[1 - part],
            send_sem=hzs_sem.at[part], recv_sem=hzr_sem.at[1 - part],
            device_id={"depth": peer}, device_id_type=MESH)

    def y_copy(part, peer):
        return pltpu.make_async_remote_copy(
            src_ref=hy_send.at[part], dst_ref=hy_recv.at[1 - part],
            send_sem=hys_sem.at[part], recv_sem=hyr_sem.at[1 - part],
            device_id={"lat": peer}, device_id_type=MESH)

    z_down, z_up = z_copy(0, me - 1), z_copy(1, me + 1)
    y_down, y_up = y_copy(0, lat - 1), y_copy(1, lat + 1)
    sides = ((me > 0, z_down), (me < n - 1, z_up), (lat > 0, y_down), (lat < lats - 1, y_up))
    for there, copy in sides:
        pl.when(there)(copy.start)

    for c in range(cols):
        piece = vpad[pl.ds(1, zs), pl.ds(PAD, ys), pl.ds(c * width, width)].reshape(zy, width)
        vol_t[
            pl.ds((c // group) * width, width), pl.ds((c % group) * zy, zy)
        ] = piece.astype(BF16).T

    lane = lax.broadcasted_iota(jnp.int32, (1, cap), 1)
    lo_ids = lax.broadcasted_iota(jnp.int32, (lo_size, step), 0).astype(F32).astype(BF16)
    det_ids = lax.broadcasted_iota(jnp.int32, (dets, step), 0).astype(F32).astype(BF16)
    one = jnp.ones((), BF16)
    zero = jnp.zeros((), BF16)

    def entry_rows(angle):
        src = src_ref[pl.ds(angle, 1), :]
        col = lax.rem(src, cols)
        scale = jnp.where(lane < count_ref[0, 0, angle], weight_ref[pl.ds(angle, 1), :], 0.0)
        return src, col, scale

    def forward_angle(angle):
        src, col, scale = entry_rows(angle)
        lo = (lax.rem(col, group) * zy + lax.div(src, cols)).astype(F32).astype(BF16)
        high = lax.div(col, group)
        dst = dst_ref[pl.ds(angle, 1), :]
        det = (lax.rem(dst, cols) * rows + lax.div(dst, cols)).astype(F32).astype(BF16)
        total = jnp.zeros((dets, width), F32)
        for t in range(tiles):
            at = slice(t * step, (t + 1) * step)
            lo_mat = jnp.where(lo_ids == lo[:, at], one, zero)
            det_mat = jnp.where(det_ids == det[:, at], one, zero)
            lo_hot[angle, :, at] = lo_mat
            det_hot[angle, :, at] = det_mat
            every = jnp.dot(vol_t[...], lo_mat, preferred_element_type=F32)
            picked = every[:width]
            for h in range(1, heights):
                picked = jnp.where(high[:, at] == h, every[h * width:(h + 1) * width], picked)
            scaled = (picked * scale[:, at]).astype(BF16)
            total = total + lax.dot_general(det_mat, scaled, NT, preferred_element_type=F32)
        return total.astype(BF16)

    def g_copy(s):
        peer = lax.rem(me + s, n)
        return pltpu.make_async_remote_copy(
            src_ref=gsend.at[peer], dst_ref=gbuf.at[me],
            send_sem=gs_sem.at[peer], recv_sem=gr_sem.at[me],
            device_id={"depth": peer}, device_id_type=MESH)

    @pl.loop(1, n)
    def _(s):
        peer = lax.rem(me + s, n)
        for i in range(own):
            gsend[peer, i] = forward_angle(peer * own + i)
        g_copy(s).start()

    for i in range(own):
        gbuf[me, i] = forward_angle(me * own + i)

    for there, copy in ((me < n - 1, z_down), (me > 0, z_up), (lat < lats - 1, y_down), (lat > 0, y_up)):
        pl.when(there)(copy.wait_recv)
    vpad[0, pl.ds(PAD, ys), :] = jnp.where(me > 0, hz_recv[0].astype(F32), 0.0)
    vpad[zs + 1, pl.ds(PAD, ys), :] = jnp.where(me < n - 1, hz_recv[1].astype(F32), 0.0)
    vpad[pl.ds(1, zs), PAD - 1, :] = jnp.where(lat > 0, hy_recv[0].astype(F32), 0.0)
    vpad[pl.ds(1, zs), PAD + ys, :] = jnp.where(lat < lats - 1, hy_recv[1].astype(F32), 0.0)
    first = lax.broadcasted_iota(jnp.int32, (8, xs), 1) == 0
    last = lax.broadcasted_iota(jnp.int32, (8, width), 1) == width - 1
    for y in range(0, ys, 8):
        cells = vpad[1, pl.ds(PAD + y, 8), :]
        face = slope_of(cells - vpad[0, pl.ds(PAD + y, 8), :])
        for z in range(zs):
            above = vpad[z + 2, pl.ds(PAD + y, 8), :]
            next_face = slope_of(above - cells)
            smooth = face - next_face
            smooth = smooth + slope_of(cells - vpad[z + 1, pl.ds(PAD + y - 1, 8), :])
            smooth = smooth - slope_of(vpad[z + 1, pl.ds(PAD + y + 1, 8), :] - cells)
            left = slope_of(cells - jnp.where(first, 0.0, pltpu.roll(cells, 1, 1)))
            right = pltpu.roll(left, xs - 1, 1)
            edge = jnp.where(last, slope_of(-cells[:, xs - width:]), right[:, xs - width:])
            right = jnp.concatenate([right[:, :xs - width], edge], axis=1)
            smooth = smooth + left - right
            pre[z, pl.ds(y, 8), :] = cells - (STEP_SIZE * TV_WEIGHT) * smooth
            cells, face = above, next_face

    @pl.loop(1, n)
    def _(s):
        source = lax.rem(me + s, n)
        pltpu.make_async_remote_copy(
            src_ref=gsend.at[source], dst_ref=gbuf.at[source],
            send_sem=gs_sem.at[source], recv_sem=gr_sem.at[source],
            device_id={"depth": source}, device_id_type=MESH).wait_recv()

    for i in range(own):
        kern = kern_ref[me * own + i]
        total = jnp.zeros((dets, width), F32)
        for s in range(n):
            total = total + jnp.dot(gbuf[s, i], kern, preferred_element_type=F32)
        seen = jnp.concatenate(
            [meas_ref[i, :, c * width:(c + 1) * width] for c in range(cols)], axis=0)
        residual = total - seen
        for c in range(cols):
            res_ref[i, :, c * width:(c + 1) * width] = residual[c * rows:(c + 1) * rows]
        back = lax.dot_general(kern, residual.astype(BF16), NT, preferred_element_type=F32)
        bbuf[me, i] = back.astype(BF16)

    def b_copy(s):
        peer = lax.rem(me + s, n)
        return pltpu.make_async_remote_copy(
            src_ref=bbuf.at[me], dst_ref=bbuf.at[me],
            send_sem=bs_sem.at[peer], recv_sem=br_sem.at[me],
            device_id={"depth": peer}, device_id_type=MESH)

    @pl.loop(1, n)
    def _(s):
        b_copy(s).start()

    def adjoint_angle(owner, i):
        angle = owner * own + i
        _, col, scale = entry_rows(angle)
        high = lax.div(col, group).astype(F32).astype(BF16)
        for t in range(tiles):
            at = slice(t * step, (t + 1) * step)
            rows_t = jnp.dot(bbuf[owner, i], det_hot[angle, :, at], preferred_element_type=F32)
            rows_t = (rows_t * scale[:, at]).astype(BF16)
            for h in range(heights):
                wide[h * width:(h + 1) * width, at] = jnp.where(high[:, at] == h, rows_t, zero)
        return lax.dot_general(wide[...], lo_hot[angle], NT, preferred_element_type=F32)

    adj_t[...] = adjoint_angle(me, 0)
    for i in range(1, own):
        adj_t[...] += adjoint_angle(me, i)

    @pl.loop(1, n)
    def _(s):
        source = lax.rem(me + s, n)
        pltpu.make_async_remote_copy(
            src_ref=bbuf.at[source], dst_ref=bbuf.at[source],
            send_sem=bs_sem.at[source], recv_sem=br_sem.at[source],
            device_id={"depth": source}, device_id_type=MESH).wait_recv()
        for i in range(own):
            adj_t[...] += adjoint_angle(source, i)

    stores = []
    for h in range(heights):
        for j in range(group):
            c = h * group + j
            at = pl.ds(c * width, width)
            part = adj_t[h * width:(h + 1) * width, j * zy:(j + 1) * zy].T
            outv[:, :, at] = pre[:, :, at] - STEP_SIZE * part.reshape(zs, ys, width)
        at = pl.ds(h * group * width, group * width)
        stores.append(pltpu.make_async_copy(outv.at[:, :, at], out_hbm.at[:, :, at], out_sem.at[h]))
        stores[-1].start()

    @pl.loop(1, n)
    def _(s):
        g_copy(s).wait_send()
        b_copy(s).wait_send()

    for there, copy in sides:
        pl.when(there)(copy.wait_send)
    for store in stores:
        store.wait()


def per_device(volume, measured, kernels, src_block, dst_block, path_weight, block_counts):
    n = lax.axis_size("depth")
    zs, ys, xs = volume.shape
    own, rows, _ = measured.shape
    angles, width, _ = kernels.shape
    cap = src_block.shape[3]
    cols = xs // width
    dets = rows * cols
    zy = zs * ys
    group = max(1, min(cols, 256 // zy))
    lo_size = group * zy
    heights = cols // group
    vmem = pl.BlockSpec(memory_space=pltpu.VMEM)
    dma = pltpu.SemaphoreType.DMA
    updated, residual = pl.pallas_call(
        body,
        out_shape=(
            jax.ShapeDtypeStruct(volume.shape, F32),
            jax.ShapeDtypeStruct(measured.shape, F32),
        ),
        in_specs=[pl.BlockSpec(memory_space=pl.ANY)] + [vmem] * 5
        + [pl.BlockSpec(memory_space=pltpu.SMEM)],
        out_specs=(pl.BlockSpec(memory_space=pl.ANY), vmem),
        scratch_shapes=[
            pltpu.VMEM((zs + 2, ys + 2 * PAD, xs), F32),
            pltpu.VMEM((heights * width, lo_size), BF16),
            pltpu.VMEM((angles, lo_size, cap), BF16),
            pltpu.VMEM((angles, dets, cap), BF16),
            pltpu.VMEM((n, own, dets, width), BF16),
            pltpu.VMEM((n, own, dets, width), BF16),
            pltpu.VMEM((n, own, width, dets), BF16),
            pltpu.VMEM((heights * width, cap), BF16),
            pltpu.VMEM((heights * width, lo_size), F32),
            pltpu.VMEM((zs, ys, xs), F32),
            pltpu.VMEM((zs, ys, xs), F32),
            pltpu.VMEM((2, ys, xs), BF16),
            pltpu.VMEM((2, ys, xs), BF16),
            pltpu.VMEM((2, zs, xs), BF16),
            pltpu.VMEM((2, zs, xs), BF16),
            dma, dma((heights,)), dma((n,)), dma((n,)), dma((n,)), dma((n,)),
            dma((2,)), dma((2,)), dma((2,)), dma((2,)),
        ],
        compiler_params=pltpu.CompilerParams(
            collective_id=0, has_side_effects=True, vmem_limit_bytes=60 * 1024 * 1024),
        name="tomo_step",
    )(
        volume, measured, kernels, src_block.reshape(angles, cap), dst_block.reshape(angles, cap),
        path_weight.reshape(angles, cap), block_counts,
    )
    return (updated, residual)


def solution(mesh):
    placed = (
        P("depth", "lat", None),
        P("depth", "lat", None),
        P(),
        P("depth", "lat", None, None),
        P("depth", "lat", None, None),
        P("depth", "lat", None, None),
        P("depth", "lat", None),
    )
    return jax.shard_map(
        per_device,
        mesh=mesh,
        in_specs=placed,
        out_specs=(P("depth", "lat", None), P("depth", "lat", None)),
        check_vma=False,
    )
```

```python
import functools

import jax
import jax.numpy as jnp
from jax import lax
from jax.experimental import pallas as pl
from jax.experimental.pallas import tpu as pltpu
from jax.sharding import PartitionSpec as P

SMOOTH_EPS = 0.1
STEP_SIZE = 0.1
TV_WEIGHT = 0.5
F32 = jnp.float32
BF16 = jnp.bfloat16
MESH = pl.DeviceIdType.MESH
NT = (((1,), (1,)), ((), ()))
TN = (((0,), (0,)), ((), ()))
PAD = 8


def slope_of(change):
    return change * lax.rsqrt(change * change + SMOOTH_EPS * SMOOTH_EPS)


def body(
    vol_hbm, meas_ref, kern_ref, src_ref, dst_ref, weight_ref, count_ref,
    out_hbm, res_ref,
    vpad, vol_t, lo_hot, det_hot, gsend, gbuf, bbuf, wide, adj_t, pre, outv,
    hz_send, hz_recv, hy_send, hy_recv,
    in_sem, out_sem, gs_sem, gr_sem, bs_sem, br_sem, hzs_sem, hzr_sem, hys_sem, hyr_sem,
):
    n = lax.axis_size("depth")
    lats = lax.axis_size("lat")
    me = lax.axis_index("depth")
    lat = lax.axis_index("lat")
    zs, ys, xs = outv.shape
    zy = zs * ys
    own, rows, _ = meas_ref.shape
    width = kern_ref.shape[1]
    cols = xs // width
    cap = src_ref.shape[1]
    lo_size = lo_hot.shape[1]
    group = lo_size // zy
    heights = cols // group
    dets = det_hot.shape[1]
    step = min(256, cap)
    tiles = cap // step

    load = pltpu.make_async_copy(vol_hbm, vpad.at[pl.ds(1, zs), pl.ds(PAD, ys), :], in_sem)
    load.start()
    barrier = pltpu.get_barrier_semaphore()

    @pl.loop(1, n)
    def _(s):
        peer = lax.rem(me + s, n)
        pl.semaphore_signal(barrier, inc=1, device_id={"depth": peer}, device_id_type=MESH)

    @pl.when(lat > 0)
    def _():
        pl.semaphore_signal(barrier, inc=1, device_id={"lat": lat - 1}, device_id_type=MESH)

    @pl.when(lat < lats - 1)
    def _():
        pl.semaphore_signal(barrier, inc=1, device_id={"lat": lat + 1}, device_id_type=MESH)

    load.wait()
    hz_send[0] = vpad[1, pl.ds(PAD, ys), :].astype(BF16)
    hz_send[1] = vpad[zs, pl.ds(PAD, ys), :].astype(BF16)
    hy_send[0] = vpad[pl.ds(1, zs), PAD, :].astype(BF16)
    hy_send[1] = vpad[pl.ds(1, zs), PAD + ys - 1, :].astype(BF16)

    beside = (lat > 0).astype(jnp.int32) + (lat < lats - 1).astype(jnp.int32)
    pl.semaphore_wait(barrier, n - 1 + beside)

    def z_copy(part, peer):
        return pltpu.make_async_remote_copy(
            src_ref=hz_send.at[part], dst_ref=hz_recv.at[1 - part],
            send_sem=hzs_sem.at[part], recv_sem=hzr_sem.at[1 - part],
            device_id={"depth": peer}, device_id_type=MESH)

    def y_copy(part, peer):
        return pltpu.make_async_remote_copy(
            src_ref=hy_send.at[part], dst_ref=hy_recv.at[1 - part],
            send_sem=hys_sem.at[part], recv_sem=hyr_sem.at[1 - part],
            device_id={"lat": peer}, device_id_type=MESH)

    z_down, z_up = z_copy(0, me - 1), z_copy(1, me + 1)
    y_down, y_up = y_copy(0, lat - 1), y_copy(1, lat + 1)
    sides = ((me > 0, z_down), (me < n - 1, z_up), (lat > 0, y_down), (lat < lats - 1, y_up))
    for there, copy in sides:
        pl.when(there)(copy.start)

    for c in range(cols):
        piece = vpad[pl.ds(1, zs), pl.ds(PAD, ys), pl.ds(c * width, width)].reshape(zy, width)
        vol_t[
            pl.ds((c // group) * width, width), pl.ds((c % group) * zy, zy)
        ] = piece.astype(BF16).T

    lane = lax.broadcasted_iota(jnp.int32, (1, cap), 1)
    lo_ids = lax.broadcasted_iota(jnp.int32, (lo_size, step), 0).astype(F32).astype(BF16)
    det_ids = lax.broadcasted_iota(jnp.int32, (dets, step), 0).astype(F32).astype(BF16)
    one = jnp.ones((), BF16)
    zero = jnp.zeros((), BF16)

    def entry_rows(angle):
        src = src_ref[pl.ds(angle, 1), :]
        col = lax.rem(src, cols)
        scale = jnp.where(lane < count_ref[0, 0, angle], weight_ref[pl.ds(angle, 1), :], 0.0)
        return src, col, scale

    def forward_angle(angle):
        src, col, scale = entry_rows(angle)
        lo = (lax.rem(col, group) * zy + lax.div(src, cols)).astype(F32).astype(BF16)
        high = lax.div(col, group)
        dst = dst_ref[pl.ds(angle, 1), :]
        det = (lax.rem(dst, cols) * rows + lax.div(dst, cols)).astype(F32).astype(BF16)
        total = jnp.zeros((width, dets), F32)
        for t in range(tiles):
            at = slice(t * step, (t + 1) * step)
            lo_mat = jnp.where(lo_ids == lo[:, at], one, zero)
            det_mat = jnp.where(det_ids == det[:, at], one, zero)
            lo_hot[angle, :, at] = lo_mat
            det_hot[angle, :, at] = det_mat
            every = jnp.dot(vol_t[...], lo_mat, preferred_element_type=F32)
            picked = every[:width]
            for h in range(1, heights):
                picked = jnp.where(high[:, at] == h, every[h * width:(h + 1) * width], picked)
            scaled = (picked * scale[:, at]).astype(BF16)
            total = total + lax.dot_general(scaled, det_mat, NT, preferred_element_type=F32)
        return total.astype(BF16)

    def g_copy(s):
        peer = lax.rem(me + s, n)
        return pltpu.make_async_remote_copy(
            src_ref=gsend.at[peer], dst_ref=gbuf.at[me],
            send_sem=gs_sem.at[peer], recv_sem=gr_sem.at[me],
            device_id={"depth": peer}, device_id_type=MESH)

    def take_halo():
        for there, copy in ((me < n - 1, z_down), (me > 0, z_up), (lat < lats - 1, y_down), (lat > 0, y_up)):
            pl.when(there)(copy.wait_recv)
        vpad[0, pl.ds(PAD, ys), :] = jnp.where(me > 0, hz_recv[0].astype(F32), 0.0)
        vpad[zs + 1, pl.ds(PAD, ys), :] = jnp.where(me < n - 1, hz_recv[1].astype(F32), 0.0)
        vpad[pl.ds(1, zs), PAD - 1, :] = jnp.where(lat > 0, hy_recv[0].astype(F32), 0.0)
        vpad[pl.ds(1, zs), PAD + ys, :] = jnp.where(lat < lats - 1, hy_recv[1].astype(F32), 0.0)

    first = lax.broadcasted_iota(jnp.int32, (8, xs), 1) == 0
    last = lax.broadcasted_iota(jnp.int32, (8, width), 1) == width - 1

    def smooth_rows(y):
        cells = vpad[1, pl.ds(PAD + y, 8), :]
        face = slope_of(cells - vpad[0, pl.ds(PAD + y, 8), :])
        for z in range(zs):
            above = vpad[z + 2, pl.ds(PAD + y, 8), :]
            next_face = slope_of(above - cells)
            smooth = face - next_face
            smooth = smooth + slope_of(cells - vpad[z + 1, pl.ds(PAD + y - 1, 8), :])
            smooth = smooth - slope_of(vpad[z + 1, pl.ds(PAD + y + 1, 8), :] - cells)
            left = slope_of(cells - jnp.where(first, 0.0, pltpu.roll(cells, 1, 1)))
            right = pltpu.roll(left, xs - 1, 1)
            edge = jnp.where(last, slope_of(-cells[:, xs - width:]), right[:, xs - width:])
            right = jnp.concatenate([right[:, :xs - width], edge], axis=1)
            smooth = smooth + left - right
            pre[z, pl.ds(y, 8), :] = cells - (STEP_SIZE * TV_WEIGHT) * smooth
            cells, face = above, next_face


    def forward_peer(s):
        peer = lax.rem(me + s, n)
        for i in range(own):
            gsend[peer, i] = forward_angle(peer * own + i)
        g_copy(s).start()

    bands = list(range(0, ys, 8))
    if n <= 4:
        for s in range(1, n):
            forward_peer(s)
    else:
        pl.loop(1, n)(forward_peer)
    take_halo()
    if bands:
        smooth_rows(bands.pop())

    for i in range(own):
        gbuf[me, i] = forward_angle(me * own + i)

    @pl.loop(1, n)
    def _(s):
        source = lax.rem(me + s, n)
        pltpu.make_async_remote_copy(
            src_ref=gsend.at[source], dst_ref=gbuf.at[source],
            send_sem=gs_sem.at[source], recv_sem=gr_sem.at[source],
            device_id={"depth": source}, device_id_type=MESH).wait_recv()

    for i in range(own):
        kern = kern_ref[me * own + i]
        total = jnp.zeros((width, dets), F32)
        for s in range(n):
            total = total + lax.dot_general(kern, gbuf[s, i], TN, preferred_element_type=F32)
        seen = jnp.concatenate(
            [meas_ref[i, :, c * width:(c + 1) * width] for c in range(cols)], axis=0)
        residual = total - seen.T
        back = jnp.dot(kern, residual.astype(BF16), preferred_element_type=F32)
        bbuf[me, i] = back.astype(BF16)
        blocks = residual.T
        for c in range(cols):
            res_ref[i, :, c * width:(c + 1) * width] = blocks[c * rows:(c + 1) * rows]

    def b_copy(s):
        peer = lax.rem(me + s, n)
        return pltpu.make_async_remote_copy(
            src_ref=bbuf.at[me], dst_ref=bbuf.at[me],
            send_sem=bs_sem.at[peer], recv_sem=br_sem.at[me],
            device_id={"depth": peer}, device_id_type=MESH)

    @pl.loop(1, n)
    def _(s):
        b_copy(s).start()

    def adjoint_angle(owner, i):
        angle = owner * own + i
        _, col, scale = entry_rows(angle)
        high = lax.div(col, group).astype(F32).astype(BF16)
        for t in range(tiles):
            at = slice(t * step, (t + 1) * step)
            rows_t = jnp.dot(bbuf[owner, i], det_hot[angle, :, at], preferred_element_type=F32)
            rows_t = (rows_t * scale[:, at]).astype(BF16)
            for h in range(heights):
                wide[h * width:(h + 1) * width, at] = jnp.where(high[:, at] == h, rows_t, zero)
        return lax.dot_general(wide[...], lo_hot[angle], NT, preferred_element_type=F32)

    if bands:
        smooth_rows(bands.pop())
    adj_t[...] = adjoint_angle(me, 0)
    for i in range(1, own):
        adj_t[...] += adjoint_angle(me, i)

    def adjoint_peer(s):
        source = lax.rem(me + s, n)
        pltpu.make_async_remote_copy(
            src_ref=bbuf.at[source], dst_ref=bbuf.at[source],
            send_sem=bs_sem.at[source], recv_sem=br_sem.at[source],
            device_id={"depth": source}, device_id_type=MESH).wait_recv()
        for i in range(own):
            adj_t[...] += adjoint_angle(source, i)

    if n <= 4:
        for s in range(1, n):
            if bands:
                smooth_rows(bands.pop())
            adjoint_peer(s)
    else:
        pl.loop(1, n)(adjoint_peer)
    while bands:
        smooth_rows(bands.pop())

    stores = []
    for h in range(heights):
        for j in range(group):
            c = h * group + j
            at = pl.ds(c * width, width)
            part = adj_t[h * width:(h + 1) * width, j * zy:(j + 1) * zy].T
            outv[:, :, at] = pre[:, :, at] - STEP_SIZE * part.reshape(zs, ys, width)
        at = pl.ds(h * group * width, group * width)
        stores.append(pltpu.make_async_copy(outv.at[:, :, at], out_hbm.at[:, :, at], out_sem.at[h]))
        stores[-1].start()

    @pl.loop(1, n)
    def _(s):
        g_copy(s).wait_send()
        b_copy(s).wait_send()

    for there, copy in sides:
        pl.when(there)(copy.wait_send)
    for store in stores:
        store.wait()


def per_device(volume, measured, kernels, src_block, dst_block, path_weight, block_counts):
    n = lax.axis_size("depth")
    zs, ys, xs = volume.shape
    own, rows, _ = measured.shape
    angles, width, _ = kernels.shape
    cap = src_block.shape[3]
    cols = xs // width
    dets = rows * cols
    zy = zs * ys
    group = max(1, min(cols, 256 // zy))
    lo_size = group * zy
    heights = cols // group
    vmem = pl.BlockSpec(memory_space=pltpu.VMEM)
    dma = pltpu.SemaphoreType.DMA
    updated, residual = pl.pallas_call(
        body,
        out_shape=(
            jax.ShapeDtypeStruct(volume.shape, F32),
            jax.ShapeDtypeStruct(measured.shape, F32),
        ),
        in_specs=[pl.BlockSpec(memory_space=pl.ANY)] + [vmem] * 5
        + [pl.BlockSpec(memory_space=pltpu.SMEM)],
        out_specs=(pl.BlockSpec(memory_space=pl.ANY), vmem),
        scratch_shapes=[
            pltpu.VMEM((zs + 2, ys + 2 * PAD, xs), F32),
            pltpu.VMEM((heights * width, lo_size), BF16),
            pltpu.VMEM((angles, lo_size, cap), BF16),
            pltpu.VMEM((angles, dets, cap), BF16),
            pltpu.VMEM((n, own, width, dets), BF16),
            pltpu.VMEM((n, own, width, dets), BF16),
            pltpu.VMEM((n, own, width, dets), BF16),
            pltpu.VMEM((heights * width, cap), BF16),
            pltpu.VMEM((heights * width, lo_size), F32),
            pltpu.VMEM((zs, ys, xs), F32),
            pltpu.VMEM((zs, ys, xs), F32),
            pltpu.VMEM((2, ys, xs), BF16),
            pltpu.VMEM((2, ys, xs), BF16),
            pltpu.VMEM((2, zs, xs), BF16),
            pltpu.VMEM((2, zs, xs), BF16),
            dma, dma((heights,)), dma((n,)), dma((n,)), dma((n,)), dma((n,)),
            dma((2,)), dma((2,)), dma((2,)), dma((2,)),
        ],
        compiler_params=pltpu.CompilerParams(
            collective_id=0, has_side_effects=True, vmem_limit_bytes=60 * 1024 * 1024),
        name="tomo_step",
    )(
        volume, measured, kernels, src_block.reshape(angles, cap), dst_block.reshape(angles, cap),
        path_weight.reshape(angles, cap), block_counts,
    )
    return (updated, residual)


def solution(mesh):
    placed = (
        P("depth", "lat", None),
        P("depth", "lat", None),
        P(),
        P("depth", "lat", None, None),
        P("depth", "lat", None, None),
        P("depth", "lat", None, None),
        P("depth", "lat", None),
    )
    return jax.shard_map(
        per_device,
        mesh=mesh,
        in_specs=placed,
        out_specs=(P("depth", "lat", None), P("depth", "lat", None)),
        check_vma=False,
    )
```

```python
import functools

import jax
import jax.numpy as jnp
from jax import lax
from jax.experimental import pallas as pl
from jax.experimental.pallas import tpu as pltpu
from jax.sharding import PartitionSpec as P

SMOOTH_EPS = 0.1
STEP_SIZE = 0.1
TV_WEIGHT = 0.5
F32 = jnp.float32
BF16 = jnp.bfloat16
MESH = pl.DeviceIdType.MESH
NT = (((1,), (1,)), ((), ()))
TN = (((0,), (0,)), ((), ()))
PAD = 8


def slope_of(change):
    return change * lax.rsqrt(change * change + SMOOTH_EPS * SMOOTH_EPS)


def body(
    vol_hbm, meas_ref, kern_ref, src_ref, dst_ref, weight_ref, count_ref,
    adj_t, pre, res_ref,
    vpad, vol_t, lo_hot, det_hot, gsend, gbuf, bbuf, wide,
    hz_send, hz_recv, hy_send, hy_recv,
    in_sem, gs_sem, gr_sem, bs_sem, br_sem, hzs_sem, hzr_sem, hys_sem, hyr_sem,
):
    n = lax.axis_size("depth")
    lats = lax.axis_size("lat")
    me = lax.axis_index("depth")
    lat = lax.axis_index("lat")
    zs, ys, xs = pre.shape
    zy = zs * ys
    own, rows, _ = meas_ref.shape
    width = kern_ref.shape[1]
    cols = xs // width
    cap = src_ref.shape[1]
    lo_size = lo_hot.shape[1]
    group = lo_size // zy
    heights = cols // group
    dets = det_hot.shape[1]
    step = min(256, cap)
    tiles = cap // step

    load = pltpu.make_async_copy(vol_hbm, vpad.at[pl.ds(1, zs), pl.ds(PAD, ys), :], in_sem)
    load.start()
    barrier = pltpu.get_barrier_semaphore()

    @pl.loop(1, n)
    def _(s):
        peer = lax.rem(me + s, n)
        pl.semaphore_signal(barrier, inc=1, device_id={"depth": peer}, device_id_type=MESH)

    @pl.when(lat > 0)
    def _():
        pl.semaphore_signal(barrier, inc=1, device_id={"lat": lat - 1}, device_id_type=MESH)

    @pl.when(lat < lats - 1)
    def _():
        pl.semaphore_signal(barrier, inc=1, device_id={"lat": lat + 1}, device_id_type=MESH)

    load.wait()
    hz_send[0] = vpad[1, pl.ds(PAD, ys), :].astype(BF16)
    hz_send[1] = vpad[zs, pl.ds(PAD, ys), :].astype(BF16)
    hy_send[0] = vpad[pl.ds(1, zs), PAD, :].astype(BF16)
    hy_send[1] = vpad[pl.ds(1, zs), PAD + ys - 1, :].astype(BF16)

    beside = (lat > 0).astype(jnp.int32) + (lat < lats - 1).astype(jnp.int32)
    pl.semaphore_wait(barrier, n - 1 + beside)

    def z_copy(part, peer):
        return pltpu.make_async_remote_copy(
            src_ref=hz_send.at[part], dst_ref=hz_recv.at[1 - part],
            send_sem=hzs_sem.at[part], recv_sem=hzr_sem.at[1 - part],
            device_id={"depth": peer}, device_id_type=MESH)

    def y_copy(part, peer):
        return pltpu.make_async_remote_copy(
            src_ref=hy_send.at[part], dst_ref=hy_recv.at[1 - part],
            send_sem=hys_sem.at[part], recv_sem=hyr_sem.at[1 - part],
            device_id={"lat": peer}, device_id_type=MESH)

    z_down, z_up = z_copy(0, me - 1), z_copy(1, me + 1)
    y_down, y_up = y_copy(0, lat - 1), y_copy(1, lat + 1)
    sides = ((me > 0, z_down), (me < n - 1, z_up), (lat > 0, y_down), (lat < lats - 1, y_up))
    for there, copy in sides:
        pl.when(there)(copy.start)

    for c in range(cols):
        piece = vpad[pl.ds(1, zs), pl.ds(PAD, ys), pl.ds(c * width, width)].reshape(zy, width)
        vol_t[
            pl.ds((c // group) * width, width), pl.ds((c % group) * zy, zy)
        ] = piece.astype(BF16).T

    lane = lax.broadcasted_iota(jnp.int32, (1, cap), 1)
    lo_ids = lax.broadcasted_iota(jnp.int32, (lo_size, step), 0).astype(F32).astype(BF16)
    det_ids = lax.broadcasted_iota(jnp.int32, (dets, step), 0).astype(F32).astype(BF16)
    one = jnp.ones((), BF16)
    zero = jnp.zeros((), BF16)

    def entry_rows(angle):
        src = src_ref[pl.ds(angle, 1), :]
        col = lax.rem(src, cols)
        scale = jnp.where(lane < count_ref[0, 0, angle], weight_ref[pl.ds(angle, 1), :], 0.0)
        return src, col, scale

    def forward_angle(angle):
        src, col, scale = entry_rows(angle)
        lo = (lax.rem(col, group) * zy + lax.div(src, cols)).astype(F32).astype(BF16)
        high = lax.div(col, group)
        dst = dst_ref[pl.ds(angle, 1), :]
        det = (lax.rem(dst, cols) * rows + lax.div(dst, cols)).astype(F32).astype(BF16)
        total = jnp.zeros((width, dets), F32)
        for t in range(tiles):
            at = slice(t * step, (t + 1) * step)
            lo_mat = jnp.where(lo_ids == lo[:, at], one, zero)
            det_mat = jnp.where(det_ids == det[:, at], one, zero)
            lo_hot[angle, :, at] = lo_mat
            det_hot[angle, :, at] = det_mat
            every = jnp.dot(vol_t[...], lo_mat, preferred_element_type=F32)
            picked = every[:width]
            for h in range(1, heights):
                picked = jnp.where(high[:, at] == h, every[h * width:(h + 1) * width], picked)
            scaled = (picked * scale[:, at]).astype(BF16)
            total = total + lax.dot_general(scaled, det_mat, NT, preferred_element_type=F32)
        return total.astype(BF16)

    def g_copy(s):
        peer = lax.rem(me + s, n)
        return pltpu.make_async_remote_copy(
            src_ref=gsend.at[peer], dst_ref=gbuf.at[me],
            send_sem=gs_sem.at[peer], recv_sem=gr_sem.at[me],
            device_id={"depth": peer}, device_id_type=MESH)

    def take_halo():
        for there, copy in ((me < n - 1, z_down), (me > 0, z_up), (lat < lats - 1, y_down), (lat > 0, y_up)):
            pl.when(there)(copy.wait_recv)
        vpad[0, pl.ds(PAD, ys), :] = jnp.where(me > 0, hz_recv[0].astype(F32), 0.0)
        vpad[zs + 1, pl.ds(PAD, ys), :] = jnp.where(me < n - 1, hz_recv[1].astype(F32), 0.0)
        vpad[pl.ds(1, zs), PAD - 1, :] = jnp.where(lat > 0, hy_recv[0].astype(F32), 0.0)
        vpad[pl.ds(1, zs), PAD + ys, :] = jnp.where(lat < lats - 1, hy_recv[1].astype(F32), 0.0)

    first = lax.broadcasted_iota(jnp.int32, (8, xs), 1) == 0
    last = lax.broadcasted_iota(jnp.int32, (8, width), 1) == width - 1
    top = lax.broadcasted_iota(jnp.int32, (8, xs), 0) == 0
    bottom = lax.broadcasted_iota(jnp.int32, (8, xs), 0) == 7

    def smooth_rows(band):
        y = pl.multiple_of(band * 8, 8)
        here = pl.ds(pl.multiple_of(PAD + y, 8), 8)
        before = pl.ds(pl.multiple_of(PAD + y - 8, 8), 8)
        after = pl.ds(pl.multiple_of(PAD + y + 8, 8), 8)
        cells = vpad[1, here, :]
        face = slope_of(cells - vpad[0, here, :])
        for z in range(zs):
            above = vpad[z + 2, here, :]
            next_face = slope_of(above - cells)
            smooth = face - next_face
            low = jnp.where(top, pltpu.roll(vpad[z + 1, before, :], 1, 0), pltpu.roll(cells, 1, 0))
            high = jnp.where(bottom, pltpu.roll(vpad[z + 1, after, :], 7, 0), pltpu.roll(cells, 7, 0))
            smooth = smooth + slope_of(cells - low) - slope_of(high - cells)
            left = slope_of(cells - jnp.where(first, 0.0, pltpu.roll(cells, 1, 1)))
            right = pltpu.roll(left, xs - 1, 1)
            edge = jnp.where(last, slope_of(-cells[:, xs - width:]), right[:, xs - width:])
            right = jnp.concatenate([right[:, :xs - width], edge], axis=1)
            smooth = smooth + left - right
            pre[z, pl.ds(y, 8), :] = cells - (STEP_SIZE * TV_WEIGHT) * smooth
            cells, face = above, next_face

    @pl.loop(1, n + 1)
    def _(s):
        owner = lax.rem(me + s, n)
        for i in range(own):
            gsend[owner, i] = forward_angle(owner * own + i)

        @pl.when(s < n)
        def _():
            g_copy(s).start()

    gbuf[me] = gsend[me]
    take_halo()

    @pl.loop(1, n)
    def _(s):
        source = lax.rem(me + s, n)
        pltpu.make_async_remote_copy(
            src_ref=gsend.at[source], dst_ref=gbuf.at[source],
            send_sem=gs_sem.at[source], recv_sem=gr_sem.at[source],
            device_id={"depth": source}, device_id_type=MESH).wait_recv()

    for i in range(own):
        kern = kern_ref[me * own + i]
        total = jnp.zeros((width, dets), F32)
        for s in range(n):
            total = total + lax.dot_general(kern, gbuf[s, i], TN, preferred_element_type=F32)
        seen = jnp.concatenate(
            [meas_ref[i, :, c * width:(c + 1) * width] for c in range(cols)], axis=0)
        residual = total - seen.T
        back = jnp.dot(kern, residual.astype(BF16), preferred_element_type=F32)
        bbuf[me, i] = back.astype(BF16)
        blocks = residual.T
        for c in range(cols):
            res_ref[i, :, c * width:(c + 1) * width] = blocks[c * rows:(c + 1) * rows]

    def b_copy(s):
        peer = lax.rem(me + s, n)
        return pltpu.make_async_remote_copy(
            src_ref=bbuf.at[me], dst_ref=bbuf.at[me],
            send_sem=bs_sem.at[peer], recv_sem=br_sem.at[me],
            device_id={"depth": peer}, device_id_type=MESH)

    @pl.loop(1, n)
    def _(s):
        b_copy(s).start()

    def adjoint_angle(owner, i):
        angle = owner * own + i
        _, col, scale = entry_rows(angle)
        high = lax.div(col, group).astype(F32).astype(BF16)
        for t in range(tiles):
            at = slice(t * step, (t + 1) * step)
            rows_t = jnp.dot(bbuf[owner, i], det_hot[angle, :, at], preferred_element_type=F32)
            rows_t = (rows_t * scale[:, at]).astype(BF16)
            for h in range(heights):
                wide[h * width:(h + 1) * width, at] = jnp.where(high[:, at] == h, rows_t, zero)
        return lax.dot_general(wide[...], lo_hot[angle], NT, preferred_element_type=F32)

    bands = ys // 8
    if bands != n:
        pl.loop(0, bands)(smooth_rows)
    adj_t[...] = jnp.zeros_like(adj_t)

    @pl.loop(0, n)
    def _(s):
        source = lax.rem(me + s, n)

        @pl.when(s > 0)
        def _():
            pltpu.make_async_remote_copy(
                src_ref=bbuf.at[source], dst_ref=bbuf.at[source],
                send_sem=bs_sem.at[source], recv_sem=br_sem.at[source],
                device_id={"depth": source}, device_id_type=MESH).wait_recv()

        if bands == n:
            smooth_rows(s)
        for i in range(own):
            adj_t[...] += adjoint_angle(source, i)

    @pl.loop(1, n)
    def _(s):
        g_copy(s).wait_send()
        b_copy(s).wait_send()

    for there, copy in sides:
        pl.when(there)(copy.wait_send)


def finish(adj_t, pre, res, out_any, res_out, outv, out_sem, res_sem):
    zs, ys, xs = pre.shape
    zy = zs * ys
    heights = out_sem.shape[0]
    width = adj_t.shape[0] // heights
    group = xs // width // heights
    span = group * width
    give = pltpu.make_async_copy(res, res_out, res_sem)
    give.start()
    stores = []
    for h in range(heights):
        for j in range(group):
            at = pl.ds((h * group + j) * width, width)
            part = adj_t[h * width:(h + 1) * width, j * zy:(j + 1) * zy].T
            outv[:, :, at] = pre[:, :, at] - STEP_SIZE * part.reshape(zs, ys, width)
        cut = pl.ds(h * span, span)
        stores.append(pltpu.make_async_copy(outv.at[:, :, cut], out_any.at[:, :, cut], out_sem.at[h]))
        stores[-1].start()
    for store in stores:
        store.wait()
    give.wait()


def per_device(volume, measured, kernels, src_block, dst_block, path_weight, block_counts):
    n = lax.axis_size("depth")
    zs, ys, xs = volume.shape
    own, rows, _ = measured.shape
    angles, width, _ = kernels.shape
    cap = src_block.shape[3]
    cols = xs // width
    dets = rows * cols
    zy = zs * ys
    group = max(1, min(cols, 256 // zy))
    lo_size = group * zy
    heights = cols // group
    vmem = pl.BlockSpec(memory_space=pltpu.VMEM)
    dma = pltpu.SemaphoreType.DMA
    room = (20 << 20) + 2 * angles * (lo_size + dets) * cap
    adjoint, plain, left = pl.pallas_call(
        body,
        out_shape=(
            jax.ShapeDtypeStruct((heights * width, lo_size), F32),
            jax.ShapeDtypeStruct(volume.shape, F32),
            jax.ShapeDtypeStruct(measured.shape, F32),
        ),
        in_specs=[pl.BlockSpec(memory_space=pltpu.HBM)] + [vmem] * 5
        + [pl.BlockSpec(memory_space=pltpu.SMEM)],
        out_specs=(vmem,) * 3,
        scratch_shapes=[
            pltpu.VMEM((zs + 2, ys + 2 * PAD, xs), F32),
            pltpu.VMEM((heights * width, lo_size), BF16),
            pltpu.VMEM((angles, lo_size, cap), BF16),
            pltpu.VMEM((angles, dets, cap), BF16),
            pltpu.VMEM((n, own, width, dets), BF16),
            pltpu.VMEM((n, own, width, dets), BF16),
            pltpu.VMEM((n, own, width, dets), BF16),
            pltpu.VMEM((heights * width, cap), BF16),
            pltpu.VMEM((2, ys, xs), BF16),
            pltpu.VMEM((2, ys, xs), BF16),
            pltpu.VMEM((2, zs, xs), BF16),
            pltpu.VMEM((2, zs, xs), BF16),
            dma, dma((n,)), dma((n,)), dma((n,)), dma((n,)),
            dma((2,)), dma((2,)), dma((2,)), dma((2,)),
        ],
        compiler_params=pltpu.CompilerParams(
            collective_id=0, has_side_effects=True, vmem_limit_bytes=room),
        name="tomo_step",
    )(
        volume, measured, kernels, src_block.reshape(angles, cap), dst_block.reshape(angles, cap),
        path_weight.reshape(angles, cap), block_counts,
    )
    everywhere = pl.BlockSpec(memory_space=pl.ANY)
    updated, residual = pl.pallas_call(
        finish,
        out_shape=(
            jax.ShapeDtypeStruct(volume.shape, F32),
            jax.ShapeDtypeStruct(measured.shape, F32),
        ),
        in_specs=[vmem] * 3,
        out_specs=(everywhere,) * 2,
        scratch_shapes=[
            pltpu.VMEM((zs, ys, xs), F32), dma((heights,)), dma,
        ],
        compiler_params=pltpu.CompilerParams(vmem_limit_bytes=8 << 20),
        name="tomo_finish",
    )(adjoint, plain, left)
    return (updated, residual)


def solution(mesh):
    placed = (
        P("depth", "lat", None),
        P("depth", "lat", None),
        P(),
        P("depth", "lat", None, None),
        P("depth", "lat", None, None),
        P("depth", "lat", None, None),
        P("depth", "lat", None),
    )
    return jax.shard_map(
        per_device,
        mesh=mesh,
        in_specs=placed,
        out_specs=(P("depth", "lat", None), P("depth", "lat", None)),
        check_vma=False,
    )
```

```python
import functools

import jax
import jax.numpy as jnp
from jax import lax
from jax.experimental import pallas as pl
from jax.experimental.pallas import tpu as pltpu
from jax.sharding import PartitionSpec as P

SMOOTH_EPS = 0.1
STEP_SIZE = 0.1
TV_WEIGHT = 0.5
F32 = jnp.float32
BF16 = jnp.bfloat16
MESH = pl.DeviceIdType.MESH
NT = (((1,), (1,)), ((), ()))
TN = (((0,), (0,)), ((), ()))
PAD = 8


def slope_of(change):
    return change * lax.rsqrt(change * change + SMOOTH_EPS * SMOOTH_EPS)


def body(
    vol_hbm, meas_ref, kern_ref, src_ref, dst_ref, weight_ref, count_ref,
    out_hbm, res_ref,
    vpad, vol_t, lo_hot, det_hot, gsend, gbuf, bbuf, wide, adj_t, pre, outv,
    hz_send, hz_recv, hy_send, hy_recv,
    in_sem, out_sem, gs_sem, gr_sem, bs_sem, br_sem, hzs_sem, hzr_sem, hys_sem, hyr_sem,
):
    n = lax.axis_size("depth")
    lats = lax.axis_size("lat")
    me = lax.axis_index("depth")
    lat = lax.axis_index("lat")
    zs, ys, xs = pre.shape
    zy = zs * ys
    own, rows, _ = meas_ref.shape
    width = kern_ref.shape[1]
    cols = xs // width
    cap = src_ref.shape[1]
    lo_size = lo_hot.shape[1]
    group = lo_size // zy
    heights = cols // group
    dets = det_hot.shape[1]
    step = min(256, cap)
    tiles = cap // step

    load = pltpu.make_async_copy(vol_hbm, vpad.at[pl.ds(1, zs), pl.ds(PAD, ys), :], in_sem)
    load.start()
    barrier = pltpu.get_barrier_semaphore()

    @pl.loop(1, n)
    def _(s):
        peer = lax.rem(me + s, n)
        pl.semaphore_signal(barrier, inc=1, device_id={"depth": peer}, device_id_type=MESH)

    @pl.when(lat > 0)
    def _():
        pl.semaphore_signal(barrier, inc=1, device_id={"lat": lat - 1}, device_id_type=MESH)

    @pl.when(lat < lats - 1)
    def _():
        pl.semaphore_signal(barrier, inc=1, device_id={"lat": lat + 1}, device_id_type=MESH)

    load.wait()
    hz_send[0] = vpad[1, pl.ds(PAD, ys), :].astype(BF16)
    hz_send[1] = vpad[zs, pl.ds(PAD, ys), :].astype(BF16)
    hy_send[0] = vpad[pl.ds(1, zs), PAD, :].astype(BF16)
    hy_send[1] = vpad[pl.ds(1, zs), PAD + ys - 1, :].astype(BF16)

    beside = (lat > 0).astype(jnp.int32) + (lat < lats - 1).astype(jnp.int32)
    pl.semaphore_wait(barrier, n - 1 + beside)

    def z_copy(part, peer):
        return pltpu.make_async_remote_copy(
            src_ref=hz_send.at[part], dst_ref=hz_recv.at[1 - part],
            send_sem=hzs_sem.at[part], recv_sem=hzr_sem.at[1 - part],
            device_id={"depth": peer}, device_id_type=MESH)

    def y_copy(part, peer):
        return pltpu.make_async_remote_copy(
            src_ref=hy_send.at[part], dst_ref=hy_recv.at[1 - part],
            send_sem=hys_sem.at[part], recv_sem=hyr_sem.at[1 - part],
            device_id={"lat": peer}, device_id_type=MESH)

    z_down, z_up = z_copy(0, me - 1), z_copy(1, me + 1)
    y_down, y_up = y_copy(0, lat - 1), y_copy(1, lat + 1)
    sides = ((me > 0, z_down), (me < n - 1, z_up), (lat > 0, y_down), (lat < lats - 1, y_up))
    for there, copy in sides:
        pl.when(there)(copy.start)

    for c in range(cols):
        piece = vpad[pl.ds(1, zs), pl.ds(PAD, ys), pl.ds(c * width, width)].reshape(zy, width)
        vol_t[
            pl.ds((c // group) * width, width), pl.ds((c % group) * zy, zy)
        ] = piece.astype(BF16).T

    lane = lax.broadcasted_iota(jnp.int32, (1, cap), 1)
    lo_ids = lax.broadcasted_iota(jnp.int32, (lo_size, step), 0).astype(F32).astype(BF16)
    det_ids = lax.broadcasted_iota(jnp.int32, (dets, step), 0).astype(F32).astype(BF16)
    one = jnp.ones((), BF16)
    zero = jnp.zeros((), BF16)

    def entry_rows(angle):
        src = src_ref[pl.ds(angle, 1), :]
        col = lax.rem(src, cols)
        scale = jnp.where(lane < count_ref[0, 0, angle], weight_ref[pl.ds(angle, 1), :], 0.0)
        return src, col, scale

    def forward_angle(angle):
        src, col, scale = entry_rows(angle)
        lo = (lax.rem(col, group) * zy + lax.div(src, cols)).astype(F32).astype(BF16)
        high = lax.div(col, group)
        dst = dst_ref[pl.ds(angle, 1), :]
        det = (lax.rem(dst, cols) * rows + lax.div(dst, cols)).astype(F32).astype(BF16)
        total = jnp.zeros((width, dets), F32)
        for t in range(tiles):
            at = slice(t * step, (t + 1) * step)
            lo_mat = jnp.where(lo_ids == lo[:, at], one, zero)
            det_mat = jnp.where(det_ids == det[:, at], one, zero)
            lo_hot[angle, :, at] = lo_mat
            det_hot[angle, :, at] = det_mat
            every = jnp.dot(vol_t[...], lo_mat, preferred_element_type=F32)
            picked = every[:width]
            for h in range(1, heights):
                picked = jnp.where(high[:, at] == h, every[h * width:(h + 1) * width], picked)
            scaled = (picked * scale[:, at]).astype(BF16)
            total = total + lax.dot_general(scaled, det_mat, NT, preferred_element_type=F32)
        return total.astype(BF16)

    def g_copy(s):
        peer = lax.rem(me + s, n)
        return pltpu.make_async_remote_copy(
            src_ref=gsend.at[peer], dst_ref=gbuf.at[me],
            send_sem=gs_sem.at[peer], recv_sem=gr_sem.at[me],
            device_id={"depth": peer}, device_id_type=MESH)

    def take_halo():
        for there, copy in ((me < n - 1, z_down), (me > 0, z_up), (lat < lats - 1, y_down), (lat > 0, y_up)):
            pl.when(there)(copy.wait_recv)
        vpad[0, pl.ds(PAD, ys), :] = jnp.where(me > 0, hz_recv[0].astype(F32), 0.0)
        vpad[zs + 1, pl.ds(PAD, ys), :] = jnp.where(me < n - 1, hz_recv[1].astype(F32), 0.0)
        vpad[pl.ds(1, zs), PAD - 1, :] = jnp.where(lat > 0, hy_recv[0].astype(F32), 0.0)
        vpad[pl.ds(1, zs), PAD + ys, :] = jnp.where(lat < lats - 1, hy_recv[1].astype(F32), 0.0)

    first = lax.broadcasted_iota(jnp.int32, (8, xs), 1) == 0
    last = lax.broadcasted_iota(jnp.int32, (8, width), 1) == width - 1
    top = lax.broadcasted_iota(jnp.int32, (8, xs), 0) == 0
    bottom = lax.broadcasted_iota(jnp.int32, (8, xs), 0) == 7

    def smooth_rows(band):
        y = pl.multiple_of(band * 8, 8)
        here = pl.ds(pl.multiple_of(PAD + y, 8), 8)
        before = pl.ds(pl.multiple_of(PAD + y - 8, 8), 8)
        after = pl.ds(pl.multiple_of(PAD + y + 8, 8), 8)
        cells = vpad[1, here, :]
        face = slope_of(cells - vpad[0, here, :])
        for z in range(zs):
            above = vpad[z + 2, here, :]
            next_face = slope_of(above - cells)
            smooth = face - next_face
            low = jnp.where(top, pltpu.roll(vpad[z + 1, before, :], 1, 0), pltpu.roll(cells, 1, 0))
            high = jnp.where(bottom, pltpu.roll(vpad[z + 1, after, :], 7, 0), pltpu.roll(cells, 7, 0))
            smooth = smooth + slope_of(cells - low) - slope_of(high - cells)
            left = slope_of(cells - jnp.where(first, 0.0, pltpu.roll(cells, 1, 1)))
            right = pltpu.roll(left, xs - 1, 1)
            edge = jnp.where(last, slope_of(-cells[:, xs - width:]), right[:, xs - width:])
            right = jnp.concatenate([right[:, :xs - width], edge], axis=1)
            smooth = smooth + left - right
            pre[z, pl.ds(y, 8), :] = cells - (STEP_SIZE * TV_WEIGHT) * smooth
            cells, face = above, next_face

    @pl.loop(1, n + 1)
    def _(s):
        owner = lax.rem(me + s, n)
        for i in range(own):
            gsend[owner, i] = forward_angle(owner * own + i)

        @pl.when(s < n)
        def _():
            g_copy(s).start()

    gbuf[me] = gsend[me]
    take_halo()

    @pl.loop(1, n)
    def _(s):
        source = lax.rem(me + s, n)
        pltpu.make_async_remote_copy(
            src_ref=gsend.at[source], dst_ref=gbuf.at[source],
            send_sem=gs_sem.at[source], recv_sem=gr_sem.at[source],
            device_id={"depth": source}, device_id_type=MESH).wait_recv()

    for i in range(own):
        kern = kern_ref[me * own + i]
        total = jnp.zeros((width, dets), F32)
        for s in range(n):
            total = total + lax.dot_general(kern, gbuf[s, i], TN, preferred_element_type=F32)
        seen = jnp.concatenate(
            [meas_ref[i, :, c * width:(c + 1) * width] for c in range(cols)], axis=0)
        residual = total - seen.T
        back = jnp.dot(kern, residual.astype(BF16), preferred_element_type=F32)
        bbuf[me, i] = back.astype(BF16)
        blocks = residual.T
        for c in range(cols):
            res_ref[i, :, c * width:(c + 1) * width] = blocks[c * rows:(c + 1) * rows]

    def b_copy(s):
        peer = lax.rem(me + s, n)
        return pltpu.make_async_remote_copy(
            src_ref=bbuf.at[me], dst_ref=bbuf.at[me],
            send_sem=bs_sem.at[peer], recv_sem=br_sem.at[me],
            device_id={"depth": peer}, device_id_type=MESH)

    @pl.loop(1, n)
    def _(s):
        b_copy(s).start()

    def adjoint_angle(owner, i):
        angle = owner * own + i
        _, col, scale = entry_rows(angle)
        high = lax.div(col, group).astype(F32).astype(BF16)
        for t in range(tiles):
            at = slice(t * step, (t + 1) * step)
            rows_t = jnp.dot(bbuf[owner, i], det_hot[angle, :, at], preferred_element_type=F32)
            rows_t = (rows_t * scale[:, at]).astype(BF16)
            for h in range(heights):
                wide[h * width:(h + 1) * width, at] = jnp.where(high[:, at] == h, rows_t, zero)
        return lax.dot_general(wide[...], lo_hot[angle], NT, preferred_element_type=F32)

    bands = ys // 8
    if bands != n:
        pl.loop(0, bands)(smooth_rows)
    adj_t[...] = jnp.zeros_like(adj_t)

    @pl.loop(0, n)
    def _(s):
        source = lax.rem(me + s, n)

        @pl.when(s > 0)
        def _():
            pltpu.make_async_remote_copy(
                src_ref=bbuf.at[source], dst_ref=bbuf.at[source],
                send_sem=bs_sem.at[source], recv_sem=br_sem.at[source],
                device_id={"depth": source}, device_id_type=MESH).wait_recv()

        if bands == n:
            smooth_rows(s)
        for i in range(own):
            adj_t[...] += adjoint_angle(source, i)

    stores = []
    for h in range(heights):
        for j in range(group):
            at = pl.ds((h * group + j) * width, width)
            part = adj_t[h * width:(h + 1) * width, j * zy:(j + 1) * zy].T
            outv[:, :, at] = pre[:, :, at] - STEP_SIZE * part.reshape(zs, ys, width)
        cut = pl.ds(h * group * width, group * width)
        stores.append(pltpu.make_async_copy(outv.at[:, :, cut], out_hbm.at[:, :, cut], out_sem.at[h]))
        stores[-1].start()

    @pl.loop(1, n)
    def _(s):
        g_copy(s).wait_send()
        b_copy(s).wait_send()

    for there, copy in sides:
        pl.when(there)(copy.wait_send)
    for store in stores:
        store.wait()


def per_device(volume, measured, kernels, src_block, dst_block, path_weight, block_counts):
    n = lax.axis_size("depth")
    zs, ys, xs = volume.shape
    own, rows, _ = measured.shape
    angles, width, _ = kernels.shape
    cap = src_block.shape[3]
    cols = xs // width
    dets = rows * cols
    zy = zs * ys
    group = max(1, min(cols, 256 // zy))
    lo_size = group * zy
    heights = cols // group
    vmem = pl.BlockSpec(memory_space=pltpu.VMEM)
    dma = pltpu.SemaphoreType.DMA
    room = 60 << 20
    updated, residual = pl.pallas_call(
        body,
        out_shape=(
            jax.ShapeDtypeStruct(volume.shape, F32),
            jax.ShapeDtypeStruct(measured.shape, F32),
        ),
        in_specs=[pl.BlockSpec(memory_space=pl.ANY)] + [vmem] * 5
        + [pl.BlockSpec(memory_space=pltpu.SMEM)],
        out_specs=(pl.BlockSpec(memory_space=pl.ANY), vmem),
        scratch_shapes=[
            pltpu.VMEM((zs + 2, ys + 2 * PAD, xs), F32),
            pltpu.VMEM((heights * width, lo_size), BF16),
            pltpu.VMEM((angles, lo_size, cap), BF16),
            pltpu.VMEM((angles, dets, cap), BF16),
            pltpu.VMEM((n, own, width, dets), BF16),
            pltpu.VMEM((n, own, width, dets), BF16),
            pltpu.VMEM((n, own, width, dets), BF16),
            pltpu.VMEM((heights * width, cap), BF16),
            pltpu.VMEM((heights * width, lo_size), F32),
            pltpu.VMEM((zs, ys, xs), F32),
            pltpu.VMEM((zs, ys, xs), F32),
            pltpu.VMEM((2, ys, xs), BF16),
            pltpu.VMEM((2, ys, xs), BF16),
            pltpu.VMEM((2, zs, xs), BF16),
            pltpu.VMEM((2, zs, xs), BF16),
            dma, dma((heights,)), dma((n,)), dma((n,)), dma((n,)), dma((n,)),
            dma((2,)), dma((2,)), dma((2,)), dma((2,)),
        ],
        compiler_params=pltpu.CompilerParams(
            collective_id=0, has_side_effects=True, vmem_limit_bytes=room),
        name="tomo_step",
    )(
        volume, measured, kernels, src_block.reshape(angles, cap), dst_block.reshape(angles, cap),
        path_weight.reshape(angles, cap), block_counts,
    )
    return (updated, residual)


def solution(mesh):
    placed = (
        P("depth", "lat", None),
        P("depth", "lat", None),
        P(),
        P("depth", "lat", None, None),
        P("depth", "lat", None, None),
        P("depth", "lat", None, None),
        P("depth", "lat", None),
    )
    return jax.shard_map(
        per_device,
        mesh=mesh,
        in_specs=placed,
        out_specs=(P("depth", "lat", None), P("depth", "lat", None)),
        check_vma=False,
    )
```
